32 devices in a mesh: dp: 8 (over y, x, core), mp: 4 (over z).
Axes of the slice: x: 2, y: 2, z: 4, core: 2. Of those that a mesh axis runs over, the one named last changes fastest.
Arguments:
- tokens: bfloat16 [1536, 8192], P(None, 'dp'), may hold values from -6 to 6
- gate_weight: bfloat16 [8192, 15360], P('dp', 'mp'), may hold values from -0.0625 to 0.0625
- up_weight: bfloat16 [8192, 15360], P('dp', 'mp'), may hold values from -0.0625 to 0.0625
- down_weight: bfloat16 [15360, 8192], P('mp', 'dp'), may hold values from -0.046875 to 0.046875
Outputs:
- mixed: bfloat16 [1536, 8192], P('mp', 'dp')
The draws below stay inside these ranges and needn't reach their ends.
All inputs are finite; a program needn't handle non-finite values.
Results may differ from the reference program's by a relative error of at most 0.0049.
Values may be sent and summed in bfloat16 or wider, within the bound.
No kernel may reach another device: no remote copies, remote signals or barrier semaphores. Data moves between devices by JAX's collectives and lax.ppermute only.
A program may use at most 192 MiB of HBM per device.

```python
import jax
import jax.numpy as jnp

D = 8192
FF = 15360
ROWS = 1536


def block_levels(own_key, dims, pieces, least, largest):
    gain, own = 1.0, jax.random.fold_in(own_key, 6)
    for axis_at, shards_of in pieces:
        draws = jnp.exp(jax.random.uniform(jax.random.fold_in(own, axis_at), (shards_of,), jnp.float32, least / len(pieces), largest / len(pieces)))
        gain = gain * jnp.repeat(draws, dims[axis_at] // shards_of).reshape([-1 if axis == axis_at else 1 for axis in range(len(dims))])
    return gain


def normal_values(key, extent, spread, most, split=(), held_as=jnp.bfloat16):
    gain = block_levels(key, extent, split, -0.22, 0.18) if split else 1.0
    array = jax.random.normal(key, extent, jnp.float32) * spread * gain
    return jnp.minimum(jnp.maximum(array, -most), most).astype(held_as)


def setup_inputs(seed: int = 0) -> dict:
    arg_keys = jax.random.split(jax.random.key(seed), 5)
    return {
        "tokens": normal_values(arg_keys[0], (ROWS, D), 1.0, 6.0, ((1, 8),)),
        "gate_weight": normal_values(arg_keys[1], (D, FF), D ** -0.5, 0.0625, ((0, 8), (1, 4))),
        "up_weight": normal_values(arg_keys[2], (D, FF), D ** -0.5, 0.0625, ((0, 8), (1, 4))),
        "down_weight": normal_values(arg_keys[3], (FF, D), FF ** -0.5, 0.046875, ((0, 4), (1, 8))),
    }


def reference(tokens, gate_weight, up_weight, down_weight):
    gate = jnp.dot(tokens, gate_weight, preferred_element_type=jnp.float32)
    up = jnp.dot(tokens, up_weight, preferred_element_type=jnp.float32)
    hidden = (jax.nn.silu(gate) * up).astype(jnp.bfloat16)
    mixed = jnp.dot(hidden, down_weight, preferred_element_type=jnp.float32)
    return mixed.astype(jnp.bfloat16)
```

```python
import functools

import jax
import jax.numpy as jnp
from jax import lax
from jax.experimental import pallas as pl
from jax.experimental.pallas import tpu as pltpu
from jax.sharding import PartitionSpec as P

F32, BF16 = jnp.float32, jnp.bfloat16


def tile_of(extent, most):
    return max(t for t in range(128, min(extent, most) + 1, 128) if extent % t == 0)


def project(where, t_own, t_other, weights, splits, dtype, most=640):
    rows, depth = t_own.shape
    half = weights[0][1].shape[1]
    tile = tile_of(half, most)
    steps = half // tile
    count = len(weights)

    def kernel(where_ref, a_ref, b_ref, *refs):
        w_refs, outs = refs[: 2 * count], refs[2 * count :]
        for i in range(count):
            total = jnp.dot(a_ref[...], w_refs[2 * i][...], preferred_element_type=F32)
            total += jnp.dot(b_ref[...], w_refs[2 * i + 1][...], preferred_element_type=F32)
            at = 0
            for out, size in zip(outs, splits):
                out[i] = total[at : at + size].astype(dtype)
                at += size

    whole = pl.BlockSpec((rows, depth), lambda j, w: (0, 0))
    pair = [
        pl.BlockSpec((depth, tile), lambda j, w: (0, w[0] * steps + j)),
        pl.BlockSpec((depth, tile), lambda j, w: (0, j)),
    ]
    size = jnp.dtype(dtype).itemsize
    return pl.pallas_call(
        kernel,
        out_shape=[jax.ShapeDtypeStruct((count, r, half), dtype) for r in splits],
        grid_spec=pltpu.PrefetchScalarGridSpec(
            num_scalar_prefetch=1,
            grid=(steps,),
            in_specs=[whole, whole, *(pair * count)],
            out_specs=[pl.BlockSpec((count, r, tile), lambda j, w: (0, 0, j)) for r in splits],
        ),
        cost_estimate=pl.CostEstimate(
            flops=4 * rows * depth * half * count,
            bytes_accessed=4 * depth * half * count + 4 * rows * depth + rows * half * count * size,
            transcendentals=0,
        ),
        name="project",
    )(where, t_own, t_other, *(w for both in weights for w in both))


def down(where, own, other, weight, most=256):
    _, s, half = own[0].shape
    width = weight.shape[1]
    tile = tile_of(width, most)
    count = len(own)

    def kernel(where_ref, *refs):
        pieces = refs[:count], refs[count : 2 * count]
        w_own, w_other, sent, kept = refs[2 * count : 2 * count + 4]
        held = refs[2 * count + 4 :]

        @pl.when(pl.program_id(0) == 0)
        def _():
            for side in range(2):
                for r in range(3):
                    held[side][where_ref[1] ^ r] = pieces[side][r][...]
                for chunk in range(2):
                    held[side][where_ref[1] ^ 3, chunk] = pieces[side][3 + chunk][...]

        total = jnp.dot(held[0][...].reshape(8 * s, half), w_own[...], preferred_element_type=F32)
        total += jnp.dot(held[1][...].reshape(8 * s, half), w_other[...], preferred_element_type=F32)
        total = total.reshape(4, 2, s, tile)
        for i in range(2):
            sent[i] = total[2 * i + 1].astype(sent.dtype)
            kept[i] = total[2 * i]

    three = pl.BlockSpec((2, s, half), lambda j, w: (0, 0, 0))
    two = pl.BlockSpec((s, half), lambda j, w: (0, 0))
    out = pl.BlockSpec((2, 2, s, tile), lambda j, w: (0, 0, 0, j))
    return pl.pallas_call(
        kernel,
        out_shape=[jax.ShapeDtypeStruct((2, 2, s, width), d) for d in (BF16, F32)],
        grid_spec=pltpu.PrefetchScalarGridSpec(
            num_scalar_prefetch=1,
            grid=(width // tile,),
            in_specs=[
                *([three] * 3 + [two] * 2) * 2,
                pl.BlockSpec((half, tile), lambda j, w: (w[0], j)),
                pl.BlockSpec((half, tile), lambda j, w: (1 - w[0], j)),
            ],
            out_specs=[out, out],
            scratch_shapes=[pltpu.VMEM((4, 2, s, half), BF16)] * 2,
        ),
        cost_estimate=pl.CostEstimate(
            flops=32 * s * half * width,
            bytes_accessed=4 * half * width + 32 * s * half + 24 * s * width,
            transcendentals=0,
        ),
        name="down",
    )(where, *own, *other, weight, weight)


def chunked(tokens, gate_weight, up_weight, down_weight, shares):
    rows, depth = tokens.shape
    half = gate_weight.shape[1] // 2
    block = rows // 4
    me, z = lax.axis_index("dp"), lax.axis_index("mp")
    core, chip = me % 2, me // 2
    where = jnp.stack([core, z ^ chip])

    def along(axis, bit, value):
        count = lax.axis_size(axis)
        return lax.ppermute(value, axis, [(i, i ^ bit) for i in range(count)])

    over_core = functools.partial(along, "dp", 1)
    over_x = functools.partial(along, "dp", 2)
    over_y = functools.partial(along, "dp", 4)

    def rows_of(place, at, s):
        return lax.dynamic_slice(tokens, ((chip ^ place) * block + at, 0), (s, depth))

    starts, at = [], 0
    for s in shares:
        starts.append(at)
        at += 2 * s
    away = [
        jnp.concatenate([rows_of(3, a, s), rows_of(1, a, s), rows_of(3, a + s, s), rows_of(2, a + s, s)])
        for a, s in zip(starts, shares)
    ]
    near = [
        jnp.concatenate([rows_of(2, a, s), rows_of(1, a + s, s), rows_of(0, a, s), rows_of(0, a + s, s)])
        for a, s in zip(starts, shares)
    ]
    other_half = lambda w: lax.dynamic_slice(w, (0, (1 - core) * half), (depth, half))
    away_other = [over_core(away[0])]
    gate = (gate_weight, over_core(other_half(gate_weight)))
    up = (up_weight, over_core(other_half(up_weight)))
    near_other = [over_core(near[0])]
    for a, b in zip(away[1:], near[1:]):
        away_other.append(over_core(a))
        near_other.append(over_core(b))

    pairs = range(len(shares))
    first = []
    for p in pairs:
        s = shares[p]
        sums = []
        for weights in ([gate], [up]) if p == 0 else ([gate, up],):
            x_first, y_first = project(where, away[p], away_other[p], weights, (2 * s, 2 * s), BF16)
            sums.append((over_x(x_first), over_y(y_first)))
        first.append([jnp.concatenate(v) if len(v) > 1 else v[0] for v in zip(*sums)])
    keep = [
        project(where, near[p], near_other[p], [gate, up], (shares[p],) * 4, F32) for p in pairs
    ]
    second = []
    for p in pairs:
        s = shares[p]
        x_first, y_first = first[p]
        via_y = over_y((keep[p][0] + x_first[:, :s].astype(F32)).astype(BF16))
        via_x = over_x((keep[p][1] + y_first[:, :s].astype(F32)).astype(BF16))
        second.append((via_y, via_x))
    outs = []
    for p in pairs:
        s = shares[p]
        parts = []
        for chunk in range(2):
            total = keep[p][2 + chunk] + first[p][chunk][:, s:].astype(F32)
            total += second[p][chunk].astype(F32)
            parts.append((jax.nn.silu(total[0]) * total[1]).astype(BF16))
        mine = jnp.stack(parts)
        from_x, from_y = over_x(mine), over_y(mine)
        own = [mine, from_x, from_y, over_x(from_y[0]), over_y(from_x[1])]
        sent, kept = down(where, own, [over_core(v) for v in own], down_weight)
        got = along("mp", 1, sent)
        passed = along("mp", 2, (kept[1] + got[1].astype(F32)).astype(BF16))
        out = kept[0] + got[0].astype(F32) + passed.astype(F32)
        outs.append(out.astype(BF16).reshape(2 * s, -1))
    return jnp.concatenate(outs)


def plain(tokens, gate_weight, up_weight, down_weight):
    group = gate_weight.shape[1]
    both_weights = jnp.concatenate((gate_weight, up_weight), axis=1)
    summed = lax.psum_scatter(
        jnp.dot(tokens, both_weights, preferred_element_type=F32), "dp", scatter_dimension=0, tiled=True
    )
    hidden = (jax.nn.silu(summed[:, :group]) * summed[:, group:]).astype(BF16)
    partial_out = jnp.dot(
        lax.all_gather(hidden, "dp", axis=0, tiled=True), down_weight, preferred_element_type=F32
    )
    mixed = lax.psum_scatter(partial_out, "mp", scatter_dimension=0, tiled=True)
    return mixed.astype(BF16)


def body(tokens, gate_weight, up_weight, down_weight):
    args = tokens, gate_weight, up_weight, down_weight
    if lax.axis_size("dp") == 8 and lax.axis_size("mp") == 4 and tokens.shape[0] % 256 == 0:
        part = tokens.shape[0] // 16
        return chunked(*args, (part, part))
    return plain(*args)


def solution(mesh):
    in_specs = (P(None, "dp"), P("dp", "mp"), P("dp", "mp"), P("mp", "dp"))
    out_specs = P("mp", "dp")
    return jax.shard_map(body, mesh=mesh, in_specs=in_specs, out_specs=out_specs, check_vma=False)
```

```python
import jax
import jax.numpy as jnp
from jax import lax
from jax.experimental import pallas as pl
from jax.experimental.pallas import tpu as pltpu
from jax.sharding import PartitionSpec as P


F32, BF16 = jnp.float32, jnp.bfloat16
MIB = 1 << 20
ANY = pl.BlockSpec(memory_space=pl.ANY)
VMEM = pl.BlockSpec(memory_space=pltpu.VMEM)
SMEM = pl.BlockSpec(memory_space=pltpu.SMEM)
LIMIT = 16
ALONE = 17
ROWS = 8


def tile_of(extent, most):
    return max(t for t in range(128, min(extent, most) + 1, 128) if extent % t == 0)


def gather_rows(where, tokens, lists, sizes, limit=8):
    depth = tokens.shape[1]
    block = tokens.shape[0] // 4
    count = sum(map(len, lists))

    def kernel(where_ref, tokens_ref, *refs):
        outs, sems = refs[:-1], refs[-1]
        copies = []
        for out, places, s in zip(outs, lists, sizes):
            for n, (place, at) in enumerate(places):
                first = pl.multiple_of((where_ref[2] ^ place) * block + at, 16)
                copies.append(
                    pltpu.make_async_copy(
                        tokens_ref.at[pl.ds(first, s)], out.at[pl.ds(n * s, s)], sems.at[len(copies)]
                    )
                )
        for copy in copies:
            copy.start()
        for copy in copies:
            copy.wait()

    return pl.pallas_call(
        kernel,
        out_shape=[jax.ShapeDtypeStruct((len(p) * s, depth), BF16) for p, s in zip(lists, sizes)],
        in_specs=[SMEM, ANY],
        out_specs=[VMEM] * len(lists),
        scratch_shapes=[pltpu.SemaphoreType.DMA((count,))],
        cost_estimate=pl.CostEstimate(flops=0, bytes_accessed=4 * tokens.size, transcendentals=0),
        compiler_params=pltpu.CompilerParams(vmem_limit_bytes=limit * MIB),
        name="gather_rows",
    )(where, tokens)


def halves(where, weight, cuts, limit):
    depth, half = weight.shape[0], weight.shape[1] // 2
    spans = [(0, 0, half)]
    for size in cuts:
        spans.append((1, sum(size for side, _, size in spans if side), size))

    def kernel(where_ref, w, *refs):
        sems = refs[-1]
        copies = [
            pltpu.make_async_copy(
                w.at[:, pl.ds(pl.multiple_of((side ^ where_ref[0]) * half + at, 128), size)], out, sems.at[n]
            )
            for n, (out, (side, at, size)) in enumerate(zip(refs[:-1], spans))
        ]
        for copy in copies:
            copy.start()
        for copy in copies:
            copy.wait()

    return pl.pallas_call(
        kernel,
        out_shape=[jax.ShapeDtypeStruct((depth, size), BF16) for _, _, size in spans],
        in_specs=[SMEM, ANY],
        out_specs=[VMEM] * len(spans),
        scratch_shapes=[pltpu.SemaphoreType.DMA((len(spans),))],
        cost_estimate=pl.CostEstimate(flops=0, bytes_accessed=8 * depth * half, transcendentals=0),
        compiler_params=pltpu.CompilerParams(vmem_limit_bytes=limit * MIB),
        name="halves",
    )(where, weight)


def bring(value):
    def kernel(source, out, sem):
        copy = pltpu.make_async_copy(source, out, sem)
        copy.start()
        copy.wait()

    return pl.pallas_call(
        kernel,
        out_shape=jax.ShapeDtypeStruct(value.shape, value.dtype),
        in_specs=[ANY],
        out_specs=VMEM,
        scratch_shapes=[pltpu.SemaphoreType.DMA],
        cost_estimate=pl.CostEstimate(flops=0, bytes_accessed=4 * value.size, transcendentals=0),
        compiler_params=pltpu.CompilerParams(vmem_limit_bytes=9 * MIB),
        name="bring",
    )(value)


def project(rows_own, rows_other, weights, outs_rows, dtype, most=640):
    rows, depth = rows_own.shape
    width = sum(piece.shape[1] for piece in weights[0][2])
    tile = min(tile_of(piece.shape[1], most) for _, _, pieces in weights for piece in pieces)
    count = len(weights)
    flat = [w for own, _, pieces in weights for w in (own, *pieces)]

    def kernel(a, b, *refs):
        outs = refs[len(flat) :]
        refs = list(refs[: len(flat)])
        for i, (_, start, pieces) in enumerate(weights):
            own, at = refs.pop(0), 0
            for _ in pieces:
                other = refs.pop(0)

                @pl.loop(0, other.shape[1] // tile)
                def _(j, own=own, other=other, at=at, i=i, start=start):
                    there = pl.ds(pl.multiple_of(j * tile, 128), tile)
                    here = pl.ds(pl.multiple_of(start + at + j * tile, 128), tile)
                    to = pl.ds(pl.multiple_of(at + j * tile, 128), tile)
                    total = jnp.dot(a[...], own[:, here], preferred_element_type=F32)
                    total += jnp.dot(b[...], other[:, there], preferred_element_type=F32)
                    row = 0
                    for out, size in zip(outs, outs_rows):
                        out[i, :, to] = total[row : row + size].astype(dtype)
                        row += size

                at += other.shape[1]

    size = jnp.dtype(dtype).itemsize
    return pl.pallas_call(
        kernel,
        out_shape=[jax.ShapeDtypeStruct((count, r, width), dtype) for r in outs_rows],
        in_specs=[VMEM] * (2 + len(flat)),
        out_specs=[VMEM] * len(outs_rows),
        cost_estimate=pl.CostEstimate(
            flops=4 * rows * depth * width * count,
            bytes_accessed=4 * depth * width * count + 4 * rows * depth + rows * width * count * size,
            transcendentals=0,
        ),
        compiler_params=pltpu.CompilerParams(vmem_limit_bytes=LIMIT * MIB),
        name="project",
    )(rows_own, rows_other, *flat)


def add_received(keep, first, second=None, step=16):
    _, s, half = keep[0].shape
    parts = len(first[0])
    spans, at = [], 0
    for v in first[0]:
        both, _, width = v.shape
        for i in range(both):
            spans.append([(len(spans) if both == 1 else 0), i if both == 2 else 0, (at // half + i), at % half, width])
        at += both * width

    def kernel(*refs):
        keeps, refs = refs[:2], refs[2:]
        firsts, refs = (refs[:parts], refs[parts : 2 * parts]), refs[2 * parts :]
        seconds, outs = (refs[:2], refs[2:]) if second else (None, refs)

        def total(chunk, i, at):
            there = pl.ds(at + s if second else at, step)
            here = pl.ds(at, step)
            values = []
            for part, place, of, column, width in spans:
                if of == i:
                    v = keeps[chunk][i, here, column : column + width]
                    v += firsts[chunk][part][place, there, :].astype(F32)
                    if second:
                        v += seconds[chunk][i, here, column : column + width].astype(F32)
                    values.append(v)
            return jnp.concatenate(values, axis=1) if len(values) > 1 else values[0]

        @pl.loop(0, s // step)
        def _(n):
            at = pl.multiple_of(n * step, step)
            for chunk in range(2):
                sums = [total(chunk, i, at) for i in range(2)]
                if second:
                    outs[0][chunk, pl.ds(at, step), :] = (jax.nn.silu(sums[0]) * sums[1]).astype(BF16)
                else:
                    for i in range(2):
                        outs[chunk][i, pl.ds(at, step), :] = sums[i].astype(BF16)

    shape = jax.ShapeDtypeStruct((2, s, half), BF16)
    inputs = [*keep, *first[0], *first[1], *(second or ())]
    return pl.pallas_call(
        kernel,
        out_shape=shape if second else [shape, shape],
        in_specs=[VMEM] * len(inputs),
        out_specs=VMEM if second else [VMEM, VMEM],
        cost_estimate=pl.CostEstimate(
            flops=16 * s * half, bytes_accessed=28 * s * half, transcendentals=2 * s * half if second else 0
        ),
        compiler_params=pltpu.CompilerParams(vmem_limit_bytes=16 * MIB),
        name="add_received",
    )(*inputs)


def down(where, own, other, weight, direct, most=256):
    _, s, half = own[0].shape
    width = weight.shape[1]
    tile = tile_of(width, most)
    count = len(own)

    def kernel(where_ref, *refs):
        pieces = refs[:count], refs[count : 2 * count]
        w, *outs, held, held_other = refs[2 * count :]
        core, place = where_ref[0], where_ref[1]
        for side, to in enumerate((held, held_other)):
            for r, piece in enumerate(pieces[side]):
                if r < 3:
                    to[place ^ r] = piece[...]
                else:
                    to[place ^ 3, r - 3] = piece[...]

        @pl.loop(0, width // tile)
        def _(j):
            columns = pl.ds(pl.multiple_of(j * tile, 128), tile)
            w_own = w[pl.ds(pl.multiple_of(core * half, 128), half), columns]
            w_other = w[pl.ds(pl.multiple_of((1 - core) * half, 128), half), columns]
            total = jnp.dot(held[...].reshape(8 * s, half), w_own, preferred_element_type=F32)
            total += jnp.dot(held_other[...].reshape(8 * s, half), w_other, preferred_element_type=F32)
            total = total.reshape(4, 2, s, tile)
            if direct:
                for i, out in enumerate(outs):
                    out[:, :, columns] = total[(i + 1) % 4].astype(out.dtype)
            else:
                for i in range(2):
                    outs[0][i, :, :, columns] = total[2 * i + 1].astype(BF16)
                    outs[1][i, :, :, columns] = total[2 * i]

    if direct:
        shapes = [jax.ShapeDtypeStruct((2, s, width), d) for d in (BF16, BF16, BF16, F32)]
    else:
        shapes = [jax.ShapeDtypeStruct((2, 2, s, width), d) for d in (BF16, F32)]
    return pl.pallas_call(
        kernel,
        out_shape=shapes,
        in_specs=[SMEM] + [VMEM] * (2 * count + 1),
        out_specs=[VMEM] * len(shapes),
        scratch_shapes=[pltpu.VMEM((4, 2, s, half), BF16)] * 2,
        cost_estimate=pl.CostEstimate(
            flops=32 * s * half * width,
            bytes_accessed=4 * half * width + 32 * s * half + 24 * s * width,
            transcendentals=0,
        ),
        compiler_params=pltpu.CompilerParams(vmem_limit_bytes=LIMIT * MIB),
        name="down",
    )(where, *own, *other, weight)


def chunked(tokens, gate_weight, up_weight, down_weight, shares, direct=None):
    me, z = lax.axis_index("dp"), lax.axis_index("mp")
    core, chip = me % 2, me // 2
    where = jnp.stack([core, z ^ chip, chip])

    def along(axis, bit, value):
        count = lax.axis_size(axis)
        return lax.ppermute(value, axis, [(i, i ^ bit) for i in range(count)])

    def over_core(value):
        return along("dp", 1, value)

    def over_x(value):
        return along("dp", 2, value)

    def over_y(value):
        return along("dp", 4, value)

    pairs, away, near, at = range(len(shares)), [], [], 0
    for s in shares:
        b = at + s
        away.append([(3, at), (1, at), (3, b), (2, b)])
        near.append([(2, at), (1, b), (0, at), (0, b)])
        at += 2 * s
    lists, sizes = [*away, *near], [*shares, *shares]
    count = len(shares)
    groups = [("rowsa", [0]), ("rowsb", [1, count]), ("rowsc", [*range(2, count), *range(count + 1, 2 * count)])]
    rows = [None] * (2 * count)
    for name, members in groups:
        found = gather_rows(where, tokens, [lists[i] for i in members], [sizes[i] for i in members], ROWS if name == groups[0][0] else 8)
        for i, v in zip(members, found):
            rows[i] = v, over_core(v)
    away, near = rows[:count], rows[count:]
    half = gate_weight.shape[1] // 2
    begin = tile_of(half, half // 3)
    weights = []
    for i, w in enumerate((gate_weight, up_weight)):
        own, *other = halves(where, w, (half,) if i else (begin, half - begin), 17 if i else ALONE)
        other = [over_core(v) for v in other]
        weights.append((own, 0, [bring(v) for v in other]))
    (gate, _, pieces), up = weights
    first, keep = [], []
    s = shares[0]
    sums = []
    for w in ((gate, 0, pieces[:1]), (gate, begin, pieces[1:]), up):
        x_first, y_first = project(*away[0], [w], (2 * s, 2 * s), BF16)
        sums.append((over_x(x_first), over_y(y_first)))
    first.append([[v[i] for v in sums] for i in range(2)])
    for p in pairs:
        s = shares[p]
        if p:
            x_first, y_first = project(*away[p], weights, (2 * s, 2 * s), BF16)
            first.append(([over_x(x_first)], [over_y(y_first)]))
        keep.append(project(*near[p], weights, (s,) * 4, F32))

    outs = []
    for p in pairs:
        s = shares[p]
        onward = add_received(keep[p][:2], first[p])
        second = over_y(onward[0]), over_x(onward[1])
        mine = add_received(keep[p][2:], first[p], second)
        from_x, from_y = over_x(mine), over_y(mine)
        own = [mine, from_x, from_y, over_x(from_y[0]), over_y(from_x[1])]
        other = [over_core(v) for v in own]
        *sent, kept = down(where, own, other, down_weight, direct=p == direct)
        if p == direct:
            far = along("mp", 3, sent[2])
            middle = along("mp", 2, sent[1])
            out = kept + along("mp", 1, sent[0]).astype(F32) + middle.astype(F32) + far.astype(F32)
        else:
            got = along("mp", 1, sent[0])
            passed = along("mp", 2, (kept[1] + got[1].astype(F32)).astype(BF16))
            out = kept[0] + got[0].astype(F32) + passed.astype(F32)
        outs.append(out.astype(BF16).reshape(2 * s, -1))
    return jnp.concatenate(outs)


SHARES = (3,4,3,2)


def plain(tokens, gate_weight, up_weight, down_weight):
    group = gate_weight.shape[1]
    both_weights = jnp.concatenate((gate_weight, up_weight), axis=1)
    summed = lax.psum_scatter(
        jnp.dot(tokens, both_weights, preferred_element_type=F32), "dp", scatter_dimension=0, tiled=True
    )
    hidden = (jax.nn.silu(summed[:, :group]) * summed[:, group:]).astype(BF16)
    partial_out = jnp.dot(
        lax.all_gather(hidden, "dp", axis=0, tiled=True), down_weight, preferred_element_type=F32
    )
    mixed = lax.psum_scatter(partial_out, "mp", scatter_dimension=0, tiled=True)
    return mixed.astype(BF16)


def body(tokens, gate_weight, up_weight, down_weight):
    args = tokens, gate_weight, up_weight, down_weight
    if lax.axis_size("dp") == 8 and lax.axis_size("mp") == 4:
        unit = tokens.shape[0] // (8 * sum(SHARES))
        return chunked(*args, tuple(unit * share for share in SHARES))
    return plain(*args)


def solution(mesh):
    in_specs = (P(None, "dp"), P("dp", "mp"), P("dp", "mp"), P("mp", "dp"))
    out_specs = P("mp", "dp")
    return jax.shard_map(body, mesh=mesh, in_specs=in_specs, out_specs=out_specs, check_vma=False)
```

```python
import jax
import jax.numpy as jnp
from jax import lax
from jax.experimental import pallas as pl
from jax.experimental.pallas import tpu as pltpu
from jax.sharding import PartitionSpec as P


F32, BF16 = jnp.float32, jnp.bfloat16
MIB = 1 << 20
ANY = pl.BlockSpec(memory_space=pl.ANY)
HBM = pl.BlockSpec(memory_space=pltpu.HBM)
VMEM = pl.BlockSpec(memory_space=pltpu.VMEM)
SMEM = pl.BlockSpec(memory_space=pltpu.SMEM)
LIMIT = 16


def tile_of(extent, most):
    return max(t for t in range(128, min(extent, most) + 1, 128) if extent % t == 0)


def gather_rows(where, tokens, lists, sizes):
    depth = tokens.shape[1]
    block = tokens.shape[0] // 4
    count = sum(map(len, lists))

    def kernel(where_ref, tokens_ref, *refs):
        outs, sems = refs[:-1], refs[-1]
        copies = []
        for out, places, s in zip(outs, lists, sizes):
            for n, (place, at) in enumerate(places):
                first = pl.multiple_of((where_ref[2] ^ place) * block + at, 16)
                copies.append(
                    pltpu.make_async_copy(
                        tokens_ref.at[pl.ds(first, s)], out.at[pl.ds(n * s, s)], sems.at[len(copies)]
                    )
                )
        for copy in copies:
            copy.start()
        for copy in copies:
            copy.wait()

    return pl.pallas_call(
        kernel,
        out_shape=[jax.ShapeDtypeStruct((len(p) * s, depth), BF16) for p, s in zip(lists, sizes)],
        in_specs=[SMEM, HBM],
        out_specs=[VMEM] * len(lists),
        scratch_shapes=[pltpu.SemaphoreType.DMA((count,))],
        cost_estimate=pl.CostEstimate(flops=0, bytes_accessed=4 * tokens.size, transcendentals=0),
        compiler_params=pltpu.CompilerParams(vmem_limit_bytes=8 * MIB),
        name="gather_rows",
    )(where, tokens)


def columns_of(where, weight, spans, limit=17):
    depth, half = weight.shape[0], weight.shape[1] // 2

    def kernel(where_ref, w, *refs):
        sems = refs[-1]
        copies = [
            pltpu.make_async_copy(
                w.at[:, pl.ds(pl.multiple_of((side ^ where_ref[0]) * half + at, 128), size)], out, sems.at[n]
            )
            for n, (out, (side, at, size)) in enumerate(zip(refs[:-1], spans))
        ]
        for copy in copies:
            copy.start()
        for copy in copies:
            copy.wait()

    return pl.pallas_call(
        kernel,
        out_shape=[jax.ShapeDtypeStruct((depth, size), BF16) for _, _, size in spans],
        in_specs=[SMEM, HBM],
        out_specs=[VMEM] * len(spans),
        scratch_shapes=[pltpu.SemaphoreType.DMA((len(spans),))],
        cost_estimate=pl.CostEstimate(
            flops=0, bytes_accessed=4 * depth * sum(size for _, _, size in spans), transcendentals=0
        ),
        compiler_params=pltpu.CompilerParams(vmem_limit_bytes=limit * MIB),
        name="columns_of",
    )(where, weight)


def bring(value):
    def kernel(source, out, sem):
        copy = pltpu.make_async_copy(source, out, sem)
        copy.start()
        copy.wait()

    return pl.pallas_call(
        kernel,
        out_shape=jax.ShapeDtypeStruct(value.shape, value.dtype),
        in_specs=[ANY],
        out_specs=VMEM,
        scratch_shapes=[pltpu.SemaphoreType.DMA],
        cost_estimate=pl.CostEstimate(flops=0, bytes_accessed=4 * value.size, transcendentals=0),
        compiler_params=pltpu.CompilerParams(vmem_limit_bytes=9 * MIB),
        name="bring",
    )(value)


def project(rows_own, rows_other, weights, outs_rows, dtype, most=640):
    rows, depth = rows_own.shape
    width = sum(piece.shape[1] for piece in weights[0][2])
    tile = min(tile_of(piece.shape[1], most) for _, _, pieces in weights for piece in pieces)
    count = len(weights)
    flat = [w for own, _, pieces in weights for w in (own, *pieces)]

    def kernel(a, b, *refs):
        outs = refs[len(flat) :]
        refs = list(refs[: len(flat)])
        for i, (_, start, pieces) in enumerate(weights):
            own, at = refs.pop(0), 0
            for _ in pieces:
                other = refs.pop(0)

                @pl.loop(0, other.shape[1] // tile)
                def _(j, own=own, other=other, at=at, i=i, start=start):
                    there = pl.ds(pl.multiple_of(j * tile, 128), tile)
                    here = pl.ds(pl.multiple_of(start + at + j * tile, 128), tile)
                    to = pl.ds(pl.multiple_of(at + j * tile, 128), tile)
                    total = jnp.dot(a[...], own[:, here], preferred_element_type=F32)
                    total += jnp.dot(b[...], other[:, there], preferred_element_type=F32)
                    row = 0
                    for out, size in zip(outs, outs_rows):
                        out[i, :, to] = total[row : row + size].astype(dtype)
                        row += size

                at += other.shape[1]

    size = jnp.dtype(dtype).itemsize
    return pl.pallas_call(
        kernel,
        out_shape=[jax.ShapeDtypeStruct((count, r, width), dtype) for r in outs_rows],
        in_specs=[VMEM] * (2 + len(flat)),
        out_specs=[VMEM] * len(outs_rows),
        cost_estimate=pl.CostEstimate(
            flops=4 * rows * depth * width * count,
            bytes_accessed=4 * depth * width * count + 4 * rows * depth + rows * width * count * size,
            transcendentals=0,
        ),
        compiler_params=pltpu.CompilerParams(vmem_limit_bytes=LIMIT * MIB),
        name="project",
    )(rows_own, rows_other, *flat)


def add_received(keep, first, second=None, step=16):
    _, s, half = keep[0].shape
    parts = len(first[0])
    spans, at = [], 0
    for v in first[0]:
        both, _, width = v.shape
        for i in range(both):
            spans.append([(len(spans) if both == 1 else 0), i if both == 2 else 0, (at // half + i), at % half, width])
        at += both * width

    def kernel(*refs):
        keeps, refs = refs[:2], refs[2:]
        firsts, refs = (refs[:parts], refs[parts : 2 * parts]), refs[2 * parts :]
        seconds, outs = (refs[:2], refs[2:]) if second else (None, refs)

        def total(chunk, i, at):
            there = pl.ds(at + s if second else at, step)
            here = pl.ds(at, step)
            values = []
            for part, place, of, column, width in spans:
                if of == i:
                    v = keeps[chunk][i, here, column : column + width]
                    v += firsts[chunk][part][place, there, :].astype(F32)
                    if second:
                        v += seconds[chunk][i, here, column : column + width].astype(F32)
                    values.append(v)
            return jnp.concatenate(values, axis=1) if len(values) > 1 else values[0]

        @pl.loop(0, s // step)
        def _(n):
            at = pl.multiple_of(n * step, step)
            for chunk in range(2):
                sums = [total(chunk, i, at) for i in range(2)]
                if second:
                    outs[0][chunk, pl.ds(at, step), :] = (jax.nn.silu(sums[0]) * sums[1]).astype(BF16)
                else:
                    for i in range(2):
                        outs[chunk][i, pl.ds(at, step), :] = sums[i].astype(BF16)

    shape = jax.ShapeDtypeStruct((2, s, half), BF16)
    inputs = [*keep, *first[0], *first[1], *(second or ())]
    return pl.pallas_call(
        kernel,
        out_shape=shape if second else [shape, shape],
        in_specs=[VMEM] * len(inputs),
        out_specs=VMEM if second else [VMEM, VMEM],
        cost_estimate=pl.CostEstimate(
            flops=16 * s * half, bytes_accessed=28 * s * half, transcendentals=2 * s * half if second else 0
        ),
        compiler_params=pltpu.CompilerParams(vmem_limit_bytes=16 * MIB),
        name="add_received",
    )(*inputs)


def down(where, own, other, weight, direct, most=256):
    _, s, half = own[0].shape
    width = weight.shape[1]
    tile = tile_of(width, most)
    count = len(own)

    def kernel(where_ref, *refs):
        pieces = refs[:count], refs[count : 2 * count]
        w, *outs, held, held_other = refs[2 * count :]
        core, place = where_ref[0], where_ref[1]
        for side, to in enumerate((held, held_other)):
            for r, piece in enumerate(pieces[side]):
                if r < 3:
                    to[place ^ r] = piece[...]
                else:
                    to[place ^ 3, r - 3] = piece[...]

        @pl.loop(0, width // tile)
        def _(j):
            columns = pl.ds(pl.multiple_of(j * tile, 128), tile)
            w_own = w[pl.ds(pl.multiple_of(core * half, 128), half), columns]
            w_other = w[pl.ds(pl.multiple_of((1 - core) * half, 128), half), columns]
            total = jnp.dot(held[...].reshape(8 * s, half), w_own, preferred_element_type=F32)
            total += jnp.dot(held_other[...].reshape(8 * s, half), w_other, preferred_element_type=F32)
            total = total.reshape(4, 2, s, tile)
            if direct:
                for i, out in enumerate(outs):
                    out[:, :, columns] = total[(i + 1) % 4].astype(out.dtype)
            else:
                for i in range(2):
                    outs[0][i, :, :, columns] = total[2 * i + 1].astype(BF16)
                    outs[1][i, :, :, columns] = total[2 * i]

    if direct:
        shapes = [jax.ShapeDtypeStruct((2, s, width), d) for d in (BF16, BF16, BF16, F32)]
    else:
        shapes = [jax.ShapeDtypeStruct((2, 2, s, width), d) for d in (BF16, F32)]
    return pl.pallas_call(
        kernel,
        out_shape=shapes,
        in_specs=[SMEM] + [VMEM] * (2 * count + 1),
        out_specs=[VMEM] * len(shapes),
        scratch_shapes=[pltpu.VMEM((4, 2, s, half), BF16)] * 2,
        cost_estimate=pl.CostEstimate(
            flops=32 * s * half * width,
            bytes_accessed=4 * half * width + 32 * s * half + 24 * s * width,
            transcendentals=0,
        ),
        compiler_params=pltpu.CompilerParams(vmem_limit_bytes=LIMIT * MIB),
        name="down",
    )(where, *own, *other, weight)


def chunked(tokens, gate_weight, up_weight, down_weight, shares):
    me, z = lax.axis_index("dp"), lax.axis_index("mp")
    core, chip = me % 2, me // 2
    where = jnp.stack([core, z ^ chip, chip])

    def along(axis, bit, value):
        count = lax.axis_size(axis)
        return lax.ppermute(value, axis, [(i, i ^ bit) for i in range(count)])

    def over_core(value):
        return along("dp", 1, value)

    def over_x(value):
        return along("dp", 2, value)

    def over_y(value):
        return along("dp", 4, value)

    pairs, away, near, at = range(len(shares)), [], [], 0
    for s in shares:
        b = at + s
        away.append([(3, at), (1, at), (3, b), (2, b)])
        near.append([(2, at), (1, b), (0, at), (0, b)])
        at += 2 * s
    lists, sizes = [*away, *near], [*shares, *shares]
    count = len(shares)
    groups = [[0], [1, count], [*range(2, count), *range(count + 1, 2 * count)]]
    rows = [None] * (2 * count)
    for members in groups:
        found = gather_rows(where, tokens, [lists[i] for i in members], [sizes[i] for i in members])
        for i, v in zip(members, found):
            rows[i] = v, over_core(v)
    away, near = rows[:count], rows[count:]
    half = gate_weight.shape[1] // 2
    begin = tile_of(half, half // 3)
    weights = []
    for i, w in enumerate((gate_weight, up_weight)):
        other = []
        if not i:
            other += columns_of(where, w, [(1, 0, begin)])
        at = sum(v.shape[1] for v in other)
        own, rest = columns_of(where, w, [(0, 0, half), (1, at, half - at)])
        other = [over_core(v) for v in [*other, rest]]
        weights.append((own, 0, [bring(v) for v in other]))
    (gate, _, pieces), up = weights
    first, keep = [], []
    s = shares[0]
    sums = []
    for w in ((gate, 0, pieces[:1]), (gate, begin, pieces[1:]), up):
        x_first, y_first = project(*away[0], [w], (2 * s, 2 * s), BF16)
        sums.append((over_x(x_first), over_y(y_first)))
    first.append([[v[i] for v in sums] for i in range(2)])
    for p in pairs:
        s = shares[p]
        if p:
            x_first, y_first = project(*away[p], weights, (2 * s, 2 * s), BF16)
            first.append(([over_x(x_first)], [over_y(y_first)]))
        keep.append(project(*near[p], weights, (s,) * 4, F32))

    outs = []
    for p in pairs:
        s = shares[p]
        onward = add_received(keep[p][:2], first[p])
        second = over_y(onward[0]), over_x(onward[1])
        mine = add_received(keep[p][2:], first[p], second)
        from_x, from_y = over_x(mine), over_y(mine)
        own = [mine, from_x, from_y, over_x(from_y[0]), over_y(from_x[1])]
        other = [over_core(v) for v in own]
        *sent, kept = down(where, own, other, down_weight, direct=p in DIRECT)
        if p in DIRECT:
            far = along("mp", 3, sent[2])
            middle = along("mp", 2, sent[1])
            out = kept + along("mp", 1, sent[0]).astype(F32) + middle.astype(F32) + far.astype(F32)
        else:
            got = along("mp", 1, sent[0])
            passed = along("mp", 2, (kept[1] + got[1].astype(F32)).astype(BF16))
            out = kept[0] + got[0].astype(F32) + passed.astype(F32)
        outs.append(out.astype(BF16).reshape(2 * s, -1))
    return jnp.concatenate(outs)


SHARES = (3, 4, 3, 2)
DIRECT = (2, 3)


def plain(tokens, gate_weight, up_weight, down_weight):
    group = gate_weight.shape[1]
    both_weights = jnp.concatenate((gate_weight, up_weight), axis=1)
    summed = lax.psum_scatter(
        jnp.dot(tokens, both_weights, preferred_element_type=F32), "dp", scatter_dimension=0, tiled=True
    )
    hidden = (jax.nn.silu(summed[:, :group]) * summed[:, group:]).astype(BF16)
    partial_out = jnp.dot(
        lax.all_gather(hidden, "dp", axis=0, tiled=True), down_weight, preferred_element_type=F32
    )
    mixed = lax.psum_scatter(partial_out, "mp", scatter_dimension=0, tiled=True)
    return mixed.astype(BF16)


def body(tokens, gate_weight, up_weight, down_weight):
    args = tokens, gate_weight, up_weight, down_weight
    if lax.axis_size("dp") == 8 and lax.axis_size("mp") == 4:
        unit = tokens.shape[0] // (8 * sum(SHARES))
        return chunked(*args, tuple(unit * share for share in SHARES))
    return plain(*args)


def solution(mesh):
    in_specs = (P(None, "dp"), P("dp", "mp"), P("dp", "mp"), P("mp", "dp"))
    out_specs = P("mp", "dp")
    return jax.shard_map(body, mesh=mesh, in_specs=in_specs, out_specs=out_specs, check_vma=False)
```
